32 devices in a mesh: fsdp: 16 (over z, y, core), tensor: 2 (over x).
Axes of the slice: x: 2, y: 2, z: 4, core: 2. Of those that a mesh axis runs over, the one named last changes fastest.
Arguments:
- hidden: bfloat16 [256, 8192], P(None, 'fsdp'), may hold values from -128 to 128
- head_weight: bfloat16 [65536, 8192], P('tensor', 'fsdp'), may hold values from -1 to 1
- targets: int32 [256], replicated, may hold values from 0 to 65535
Outputs:
- logprob: float32 [256], replicated
- greedy_gap: float32 [256], replicated
The draws below stay inside these ranges and needn't reach their ends.
All inputs are finite; a program needn't handle non-finite values.
Results may differ from the reference program's by a relative error of at most 0.0003.
Values may be sent and summed in bfloat16 or wider, within the bound.
A program may use at most 192 MiB of HBM per device.

```python
import jax
import jax.numpy as jnp
from jax import lax

D = 8192
VOCAB = 65536
TOKENS = 256
N_TENSOR = 2


def head_row(base_key, vocab_index):
    row_values = jax.random.normal(jax.random.fold_in(jax.random.fold_in(base_key, 7), vocab_index), (D,), jnp.float32)
    return row_values / jnp.sqrt(jnp.sum(row_values * row_values))


def draw_head_weight(key, part):

    def one_row(vocab_index):
        return head_row(key, vocab_index)
    return jax.vmap(one_row)(jnp.arange(VOCAB, dtype=jnp.int32)).astype(jnp.bfloat16)


def draw_hidden(key, part):
    own_key = jax.random.fold_in(key, 11)
    subkeys = jax.random.split(own_key, 2)
    values = jax.random.normal(subkeys[1], (TOKENS, D), jnp.float32) * 3.0
    return jnp.clip(values, -128.0, 128.0).astype(jnp.bfloat16)


def set_ends(result, rng, low, largest):
    longest = result.shape.index(max(result.shape))
    spots = []
    for shift in (0, 1):
        where = [jax.random.randint(jax.random.fold_in(rng, axis), (), 0, length) for axis, length in enumerate(result.shape)]
        where[longest] = (where[longest] + shift) % result.shape[longest]
        spots.append(tuple(where))
    return result.at[spots[0]].set(low).at[spots[1]].set(largest)


def setup_inputs(seed: int = 0) -> dict:
    key_of = jax.random.split(jax.random.key(seed), 4)
    hidden = draw_hidden(jax.random.fold_in(key_of[3], 71), 0)
    head_weight = draw_head_weight(jax.random.fold_in(key_of[3], 71), 0)
    targets = set_ends(jax.random.randint(key_of[2], (TOKENS,), 0, VOCAB), jax.random.fold_in(key_of[2], 1), 0, VOCAB - 1).astype(jnp.int32)
    return dict(hidden=hidden, head_weight=head_weight, targets=targets)


def reference(hidden, head_weight, targets):
    block_rows = VOCAB // N_TENSOR
    stacked = head_weight.reshape(N_TENSOR, block_rows, D)

    def visit(state, inputs):
        peak_logit, expsum, target_logit = state
        head_block, block_index = inputs
        logits = jnp.dot(hidden, head_block.T, preferred_element_type=jnp.float32)
        vocab_ids = block_index * block_rows + jnp.arange(block_rows, dtype=jnp.int32)
        new_peak = jnp.maximum(peak_logit, jnp.max(logits, axis=1))
        expsum = expsum * jnp.exp(peak_logit - new_peak) + jnp.sum(jnp.exp(logits - new_peak[:, None]), axis=1)
        matches = vocab_ids[None, :] == targets[:, None]
        target_logit = target_logit + jnp.sum(jnp.where(matches, logits, jnp.zeros_like(logits)), axis=1)
        return (new_peak, expsum, target_logit), None

    start_state = (jnp.full((TOKENS,), -jnp.inf, jnp.float32), jnp.zeros((TOKENS,), jnp.float32), jnp.zeros((TOKENS,), jnp.float32))
    final_state, _ = lax.scan(visit, start_state, (stacked, jnp.arange(N_TENSOR, dtype=jnp.int32)))
    peak_logit, expsum, target_logit = final_state
    logprob = target_logit - peak_logit - jnp.log(expsum)
    greedy_gap = target_logit - peak_logit
    return logprob, greedy_gap
```

```python
import functools

import jax
import jax.numpy as jnp
from jax import lax
from jax.experimental import pallas as pl
from jax.experimental.pallas import tpu as pltpu
from jax.sharding import PartitionSpec as P

MESH = pl.DeviceIdType.MESH
TOP_CODE = 32000.0
LN2 = 0.6931471805599453
SUBS = 2


def encode(values, buffer):
    rows = values.shape[0]
    largest = jnp.maximum(jnp.max(jnp.abs(values), axis=0, keepdims=True), 1e-30)
    exponent = jnp.ceil(jnp.log(largest * (1.0 / TOP_CODE)) * (1.0 / LN2))
    inverse = jnp.exp(exponent * -LN2)
    codes = jnp.floor(values * inverse + 0.5)
    buffer[0:rows, :] = codes.astype(jnp.int32).astype(jnp.int16)
    tail = jnp.broadcast_to(exponent.astype(jnp.int32), (16, values.shape[1]))
    buffer[rows : rows + 16, :] = tail.astype(jnp.int16)


def decode(buffer, rows):
    tail = buffer[rows : rows + 16, :].astype(jnp.int32).astype(jnp.float32)
    step = jnp.exp(tail[0:1, :] * LN2)
    return buffer[0:rows, :].astype(jnp.int32).astype(jnp.float32) * step


def merge(first, second):
    peak_a, sum_a, target_a = first
    peak_b, sum_b, target_b = second
    peak = jnp.maximum(peak_a, peak_b)
    total = sum_a * jnp.exp(peak_a - peak) + sum_b * jnp.exp(peak_b - peak)
    return peak, total, target_a + target_b


def kernel(
    n, n_tensor, hidden_ref, targets_ref, head_ref, logprob_ref, gap_ref,
    other_hidden, own_rows, other_rows, outbox, inbox, stat_out, stat_in,
    local_sem, swap_send, swap_recv, hid_sem, ring_send, ring_recv, stat_send, stat_recv,
):
    chips = n // 2
    vocab = head_ref.shape[0]
    chunk = vocab // (4 * chips)
    sub = chunk // SUBS
    me = lax.axis_index("fsdp")
    tensor = lax.axis_index("tensor")
    core = lax.rem(me, 2)
    chip = me // 2
    side, along = lax.rem(chip, 2), chip // 2
    place = along + side * (chips - 1 - 2 * along)

    def device_at(position):
        upper = position // (chips // 2)
        at_chip = 2 * position + upper * (2 * (chips - 1 - position) + 1 - 2 * position)
        return at_chip * 2 + core

    neighbour = (
        device_at(lax.rem(place + 1, chips)),
        device_at(lax.rem(place + chips - 1, chips)),
    )
    twin = me + 1 - 2 * core

    def chunk_at(direction, step):
        if direction == 0:
            return lax.rem(place + 2 * chips - 1 - step, chips)
        return lax.rem(place + 1 + step, chips)

    def first_row(half, direction, step):
        return pl.multiple_of(
            half * (vocab // 2) + direction * (vocab // 4) + chunk_at(direction, step) * chunk,
            chunk,
        )

    def fetch(direction, step):
        return pltpu.make_async_copy(
            head_ref.at[pl.ds(first_row(core, direction, step), chunk), :],
            own_rows.at[direction, step],
            local_sem.at[direction, step],
        )

    def swap(direction, step):
        return pltpu.make_async_remote_copy(
            src_ref=head_ref.at[pl.ds(first_row(1 - core, direction, step), chunk), :],
            dst_ref=other_rows.at[direction, step],
            send_sem=swap_send.at[direction, step],
            recv_sem=swap_recv.at[direction, step],
            device_id={"fsdp": twin},
            device_id_type=MESH,
        )

    def pass_on(direction, step, part):
        return pltpu.make_async_remote_copy(
            src_ref=outbox.at[direction, step, part],
            dst_ref=inbox.at[direction, step, part],
            send_sem=ring_send.at[direction, step, part],
            recv_sem=ring_recv.at[direction, step, part],
            device_id={"fsdp": neighbour[direction]},
            device_id_type=MESH,
        )

    partners = []
    bit = 1
    while bit < n:
        partners.append({"fsdp": me + bit * (1 - 2 * lax.rem(me // bit, 2))})
        bit *= 2
    bit = 1
    while bit < n_tensor:
        partners.append({"tensor": tensor + bit * (1 - 2 * lax.rem(tensor // bit, 2))})
        bit *= 2

    @pl.loop(0, chips)
    def _(step):
        for direction in range(2):
            fetch(direction, step).start()

    barrier = pltpu.get_barrier_semaphore()
    greeted = [{"fsdp": neighbour[0]}, {"fsdp": neighbour[1]}, *partners]
    for device in greeted:
        pl.semaphore_signal(barrier, inc=1, device_id=device, device_id_type=MESH)
    pl.semaphore_wait(barrier, len(greeted))

    hidden_swap = pltpu.make_async_remote_copy(
        src_ref=hidden_ref,
        dst_ref=other_hidden,
        send_sem=hid_sem.at[0],
        recv_sem=hid_sem.at[1],
        device_id={"fsdp": twin},
        device_id_type=MESH,
    )
    hidden_swap.start()

    @pl.loop(0, chips)
    def _(step):
        for direction in range(2):
            swap(direction, step).start()

    hidden_swap.wait_recv()

    def product(direction, step, part):
        rows = pl.ds(part * sub, sub)
        contract = (((1,), (1,)), ((), ()))
        own = lax.dot_general(
            own_rows[direction, step, rows, :], hidden_ref[...], contract,
            preferred_element_type=jnp.float32,
        )
        other = lax.dot_general(
            other_rows[direction, step, rows, :], other_hidden[...], contract,
            preferred_element_type=jnp.float32,
        )
        return own + other

    def rows_ready(direction, step):
        fetch(direction, step).wait()
        swap(direction, step).wait_recv()

    for direction in range(2):
        rows_ready(direction, 0)
        for part in range(SUBS):
            encode(product(direction, 0, part), outbox.at[direction, 0, part])
            pass_on(direction, 0, part).start()

    @pl.loop(1, chips - 1)
    def _(step):
        for direction in range(2):
            rows_ready(direction, step)
        for part in range(SUBS):
            for direction in range(2):
                mine = product(direction, step, part)
                pass_on(direction, step - 1, part).wait_recv()
                mine = mine + decode(inbox.at[direction, step - 1, part], sub)
                encode(mine, outbox.at[direction, step, part])
                pass_on(direction, step, part).start()

    last = chips - 1
    for direction in range(2):
        rows_ready(direction, last)
    stats = None
    row_ids = lax.broadcasted_iota(jnp.int32, (sub, hidden_ref.shape[0]), 0)
    for part in range(SUBS):
        for direction in range(2):
            logits = product(direction, last, part)
            pass_on(direction, last - 1, part).wait_recv()
            logits = logits + decode(inbox.at[direction, last - 1, part], sub)
            start = tensor * vocab + first_row(core, direction, last) + part * sub
            hit = row_ids + start == targets_ref[...]
            peak = jnp.max(logits, axis=0, keepdims=True)
            found = (
                peak,
                jnp.sum(jnp.exp(logits - peak), axis=0, keepdims=True),
                jnp.sum(jnp.where(hit, logits, 0.0), axis=0, keepdims=True),
            )
            stats = found if stats is None else merge(stats, found)

    for stage, device in enumerate(partners):
        stat_out[stage] = jnp.zeros(stat_out.shape[1:], jnp.float32)
        for row in range(3):
            stat_out[stage, row : row + 1, :] = stats[row]
        copy = pltpu.make_async_remote_copy(
            src_ref=stat_out.at[stage],
            dst_ref=stat_in.at[stage],
            send_sem=stat_send.at[stage],
            recv_sem=stat_recv.at[stage],
            device_id=device,
            device_id_type=MESH,
        )
        copy.start()
        copy.wait()
        stats = merge(stats, tuple(stat_in[stage, row : row + 1, :] for row in range(3)))

    peak, total, target = stats
    gap = target - peak
    gap_ref[...] = gap
    logprob_ref[...] = gap - jnp.log(total)

    hidden_swap.wait_send()

    @pl.loop(0, chips)
    def _(step):
        for direction in range(2):
            swap(direction, step).wait_send()

    @pl.loop(0, chips - 1)
    def _(step):
        for direction in range(2):
            for part in range(SUBS):
                pass_on(direction, step, part).wait_send()


def solution(mesh):
    n, n_tensor = mesh.shape["fsdp"], mesh.shape["tensor"]

    def per_device(hidden, head_weight, targets):
        tokens, depth = hidden.shape
        vocab = head_weight.shape[0]
        chips = n // 2
        chunk = vocab // (4 * chips)
        sub = chunk // SUBS
        stages = (n.bit_length() - 1) + (n_tensor.bit_length() - 1)
        vmem = pl.BlockSpec(memory_space=pltpu.VMEM)
        dma = pltpu.SemaphoreType.DMA
        row = jax.ShapeDtypeStruct((1, tokens), jnp.float32)
        logprob, gap = pl.pallas_call(
            functools.partial(kernel, n, n_tensor),
            out_shape=(row, row),
            in_specs=[vmem, vmem, pl.BlockSpec(memory_space=pl.ANY)],
            out_specs=(vmem, vmem),
            scratch_shapes=[
                pltpu.VMEM((tokens, depth), hidden.dtype),
                pltpu.VMEM((2, chips, chunk, depth), head_weight.dtype),
                pltpu.VMEM((2, chips, chunk, depth), head_weight.dtype),
                pltpu.VMEM((2, chips - 1, SUBS, sub + 16, tokens), jnp.int16),
                pltpu.VMEM((2, chips - 1, SUBS, sub + 16, tokens), jnp.int16),
                pltpu.VMEM((stages, 8, tokens), jnp.float32),
                pltpu.VMEM((stages, 8, tokens), jnp.float32),
                dma((2, chips)),
                dma((2, chips)),
                dma((2, chips)),
                dma((2,)),
                dma((2, chips - 1, SUBS)),
                dma((2, chips - 1, SUBS)),
                dma((stages,)),
                dma((stages,)),
            ],
            compiler_params=pltpu.CompilerParams(
                collective_id=0, has_side_effects=True, vmem_limit_bytes=60 * 1024 * 1024
            ),
        )(hidden, targets.reshape(1, tokens), head_weight)
        return logprob.reshape(tokens), gap.reshape(tokens)

    return jax.shard_map(
        per_device,
        mesh=mesh,
        in_specs=(P(None, "fsdp"), P("tensor", "fsdp"), P()),
        out_specs=(P(), P()),
        check_vma=False,
    )
```

```python
import functools

import jax
import jax.numpy as jnp
from jax import lax
from jax.experimental import pallas as pl
from jax.experimental.pallas import tpu as pltpu
from jax.sharding import PartitionSpec as P

MESH = pl.DeviceIdType.MESH
TOP_CODE = 32000.0
LN2 = 0.6931471805599453
SUBS = 2


def encode(values, buffer):
    rows = values.shape[0]
    largest = jnp.maximum(jnp.max(jnp.abs(values), axis=0, keepdims=True), 1e-30)
    exponent = jnp.ceil(jnp.log(largest * (1.0 / TOP_CODE)) * (1.0 / LN2))
    inverse = jnp.exp(exponent * -LN2)
    codes = jnp.floor(values * inverse + 0.5)
    buffer[0:rows, :] = codes.astype(jnp.int32).astype(jnp.int16)
    tail = jnp.broadcast_to(exponent.astype(jnp.int32), (16, values.shape[1]))
    buffer[rows : rows + 16, :] = tail.astype(jnp.int16)


def decode(buffer, rows):
    tail = buffer[rows : rows + 16, :].astype(jnp.int32).astype(jnp.float32)
    step = jnp.exp(tail[0:1, :] * LN2)
    return buffer[0:rows, :].astype(jnp.int32).astype(jnp.float32) * step


def merge(first, second):
    peak_a, sum_a, target_a = first
    peak_b, sum_b, target_b = second
    peak = jnp.maximum(peak_a, peak_b)
    total = sum_a * jnp.exp(peak_a - peak) + sum_b * jnp.exp(peak_b - peak)
    return peak, total, target_a + target_b


def kernel(
    n, n_tensor, hidden_ref, targets_ref, head_ref, result_ref,
    other_hidden, own_rows, other_rows, outbox, inbox, group_stats, tensor_stats,
    local_sem, swap_send, swap_recv, hid_sem, ring_send, ring_recv,
    group_send, group_recv, tensor_send, tensor_recv,
):
    chips = n // 2
    vocab = head_ref.shape[0]
    chunk = vocab // (4 * chips)
    sub = chunk // SUBS
    me = lax.axis_index("fsdp")
    tensor = lax.axis_index("tensor")
    core = lax.rem(me, 2)
    chip = me // 2
    side, along = lax.rem(chip, 2), chip // 2
    place = along + side * (chips - 1 - 2 * along)

    def device_at(position):
        upper = position // (chips // 2)
        at_chip = 2 * position + upper * (2 * (chips - 1 - position) + 1 - 2 * position)
        return at_chip * 2 + core

    neighbour = (
        device_at(lax.rem(place + 1, chips)),
        device_at(lax.rem(place + chips - 1, chips)),
    )
    twin = me + 1 - 2 * core

    def chunk_at(direction, step):
        if direction == 0:
            return lax.rem(place + 2 * chips - 1 - step, chips)
        return lax.rem(place + 1 + step, chips)

    def first_row(half, direction, step, part):
        block = half * (vocab // 2) + direction * (vocab // 4)
        return pl.multiple_of(block + chunk_at(direction, step) * chunk + part * sub, sub)

    def fetch(direction, step, part):
        return pltpu.make_async_copy(
            head_ref.at[pl.ds(first_row(core, direction, step, part), sub), :],
            own_rows.at[direction, step, part],
            local_sem.at[direction, step, part],
        )

    def swap(direction, step, part):
        return pltpu.make_async_remote_copy(
            src_ref=head_ref.at[pl.ds(first_row(1 - core, direction, step, part), sub), :],
            dst_ref=other_rows.at[direction, step, part],
            send_sem=swap_send.at[direction, step, part],
            recv_sem=swap_recv.at[direction, step, part],
            device_id={"fsdp": twin},
            device_id_type=MESH,
        )

    def pass_on(direction, step, part):
        return pltpu.make_async_remote_copy(
            src_ref=outbox.at[direction, step, part],
            dst_ref=inbox.at[direction, step, part],
            send_sem=ring_send.at[direction, step, part],
            recv_sem=ring_recv.at[direction, step, part],
            device_id={"fsdp": neighbour[direction]},
            device_id_type=MESH,
        )

    blocks = [(direction, part) for part in range(SUBS) for direction in range(2)]

    for direction, part in blocks:
        fetch(direction, 0, part).start()

    barrier = pltpu.get_barrier_semaphore()
    greeted = [{"fsdp": twin}, {"fsdp": neighbour[0]}, {"fsdp": neighbour[1]}]
    for offset in range(1, n_tensor):
        greeted.append({"tensor": lax.rem(tensor + offset, n_tensor)})
    for device in greeted:
        pl.semaphore_signal(barrier, inc=1, device_id=device, device_id_type=MESH)
    pl.semaphore_wait(barrier, len(greeted))

    hidden_swap = pltpu.make_async_remote_copy(
        src_ref=hidden_ref,
        dst_ref=other_hidden,
        send_sem=hid_sem.at[0],
        recv_sem=hid_sem.at[1],
        device_id={"fsdp": twin},
        device_id_type=MESH,
    )
    hidden_swap.start()

    for direction, part in blocks:
        swap(direction, 0, part).start()
    hidden_swap.wait_recv()

    def product(direction, step, part):
        contract = (((1,), (1,)), ((), ()))
        own = lax.dot_general(
            own_rows[direction, step, part], hidden_ref[...], contract,
            preferred_element_type=jnp.float32,
        )
        other = lax.dot_general(
            other_rows[direction, step, part], other_hidden[...], contract,
            preferred_element_type=jnp.float32,
        )
        return own + other

    def ask(step):
        for direction, part in blocks:
            fetch(direction, step, part).start()
            swap(direction, step, part).start()

    def rows_ready(direction, step, part):
        fetch(direction, step, part).wait()
        swap(direction, step, part).wait_recv()

    for direction, part in blocks:
        rows_ready(direction, 0, part)
        encode(product(direction, 0, part), outbox.at[direction, 0, part])
        pass_on(direction, 0, part).start()
    ask(1)

    @pl.loop(1, chips - 1)
    def _(step):
        ask(step + 1)
        for direction, part in blocks:
            rows_ready(direction, step, part)
            mine = product(direction, step, part)
            pass_on(direction, step - 1, part).wait_recv()
            mine = mine + decode(inbox.at[direction, step - 1, part], sub)
            encode(mine, outbox.at[direction, step, part])
            pass_on(direction, step, part).start()

    last = chips - 1
    stats = None
    tokens = hidden_ref.shape[0]
    row_ids = lax.broadcasted_iota(jnp.int32, (sub, tokens), 0)
    for direction, part in blocks:
        rows_ready(direction, last, part)
        logits = product(direction, last, part)
        pass_on(direction, last - 1, part).wait_recv()
        logits = logits + decode(inbox.at[direction, last - 1, part], sub)
        start = tensor * vocab + first_row(core, direction, last, part)
        hit = row_ids + start == targets_ref[...]
        peak = jnp.max(logits, axis=0, keepdims=True)
        found = (
            peak,
            jnp.sum(jnp.exp(logits - peak), axis=0, keepdims=True),
            jnp.sum(jnp.where(hit, logits, 0.0), axis=0, keepdims=True),
        )
        stats = found if stats is None else merge(stats, found)

    def exchange(axis, size, index, slots, send_sem, recv_sem):
        def give(offset):
            return pltpu.make_async_remote_copy(
                src_ref=slots.at[index],
                dst_ref=slots.at[index],
                send_sem=send_sem.at[offset],
                recv_sem=recv_sem.at[index],
                device_id={axis: lax.rem(index + offset, size)},
                device_id_type=MESH,
            )

        def take(offset):
            source = lax.rem(index + offset, size)
            return pltpu.make_async_remote_copy(
                src_ref=slots.at[source],
                dst_ref=slots.at[source],
                send_sem=send_sem.at[offset],
                recv_sem=recv_sem.at[source],
                device_id={axis: source},
                device_id_type=MESH,
            )

        @pl.loop(1, size)
        def _(offset):
            give(offset).start()

        @pl.loop(1, size)
        def _(offset):
            take(offset).wait_recv()

        peaks = slots[:, 0:lines, :]
        peak = jnp.max(peaks, axis=0)
        total = jnp.sum(slots[:, lines : 2 * lines, :] * jnp.exp(peaks - peak), axis=0)
        target = jnp.sum(slots[:, 2 * lines : 3 * lines, :], axis=0)

        def finish():
            @pl.loop(1, size)
            def _(offset):
                give(offset).wait_send()

        return (peak, total, target), finish

    lanes = group_stats.shape[2]
    lines = tokens // lanes
    group_stats[me] = jnp.zeros(group_stats.shape[1:], jnp.float32)
    for which in range(3):
        for line in range(lines):
            group_stats[me, which * lines + line : which * lines + line + 1, :] = stats[which][
                :, line * lanes : (line + 1) * lanes
            ]
    stats, finish_group = exchange("fsdp", n, me, group_stats, group_send, group_recv)
    tensor_stats[tensor] = jnp.zeros(tensor_stats.shape[1:], jnp.float32)
    for which in range(3):
        tensor_stats[tensor, which * lines : (which + 1) * lines, :] = stats[which]
    stats, finish_tensor = exchange(
        "tensor", n_tensor, tensor, tensor_stats, tensor_send, tensor_recv
    )

    peak, total, target = stats
    gap = target - peak
    result_ref[0] = gap - jnp.log(total)
    result_ref[1] = gap

    finish_group()
    finish_tensor()
    hidden_swap.wait_send()

    @pl.loop(0, chips)
    def _(step):
        for direction, part in blocks:
            swap(direction, step, part).wait_send()

    @pl.loop(0, chips - 1)
    def _(step):
        for direction, part in blocks:
            pass_on(direction, step, part).wait_send()


def solution(mesh):
    n, n_tensor = mesh.shape["fsdp"], mesh.shape["tensor"]

    def per_device(hidden, head_weight, targets):
        tokens, depth = hidden.shape
        vocab = head_weight.shape[0]
        chips = n // 2
        chunk = vocab // (4 * chips)
        sub = chunk // SUBS
        lanes = min(tokens, 128)
        lines = tokens // lanes
        slot_rows = -(-3 * lines // 8) * 8
        vmem = pl.BlockSpec(memory_space=pltpu.VMEM)
        dma = pltpu.SemaphoreType.DMA
        result = pl.pallas_call(
            functools.partial(kernel, n, n_tensor),
            out_shape=jax.ShapeDtypeStruct((2, lines, lanes), jnp.float32),
            in_specs=[vmem, vmem, pl.BlockSpec(memory_space=pl.ANY)],
            out_specs=vmem,
            scratch_shapes=[
                pltpu.VMEM((tokens, depth), hidden.dtype),
                pltpu.VMEM((2, chips, SUBS, sub, depth), head_weight.dtype),
                pltpu.VMEM((2, chips, SUBS, sub, depth), head_weight.dtype),
                pltpu.VMEM((2, chips - 1, SUBS, sub + 16, tokens), jnp.int16),
                pltpu.VMEM((2, chips - 1, SUBS, sub + 16, tokens), jnp.int16),
                pltpu.VMEM((n, slot_rows, lanes), jnp.float32),
                pltpu.VMEM((n_tensor, slot_rows, lanes), jnp.float32),
                dma((2, chips, SUBS)),
                dma((2, chips, SUBS)),
                dma((2, chips, SUBS)),
                dma((2,)),
                dma((2, chips - 1, SUBS)),
                dma((2, chips - 1, SUBS)),
                dma((n,)),
                dma((n,)),
                dma((n_tensor,)),
                dma((n_tensor,)),
            ],
            compiler_params=pltpu.CompilerParams(
                collective_id=0, has_side_effects=True, vmem_limit_bytes=60 * 1024 * 1024
            ),
        )(hidden, targets.reshape(1, tokens), head_weight)
        return result[0].reshape(tokens), result[1].reshape(tokens)

    return jax.shard_map(
        per_device,
        mesh=mesh,
        in_specs=(P(None, "fsdp"), P("tensor", "fsdp"), P()),
        out_specs=(P(), P()),
        check_vma=False,
    )
```

```python
import functools

import jax
import jax.numpy as jnp
from jax import lax
from jax.experimental import pallas as pl
from jax.experimental.pallas import tpu as pltpu
from jax.sharding import PartitionSpec as P

MESH = pl.DeviceIdType.MESH
TOP_CODE = 32700.0
SUBS = 2


def encode(values, codes, steps):
    largest = jnp.maximum(jnp.max(jnp.abs(values), axis=0, keepdims=True), 1e-30)
    steps[...] = largest * (1.0 / TOP_CODE)
    scaled = jnp.floor(values * (TOP_CODE / largest) + 0.5)
    codes[...] = scaled.astype(jnp.int32).astype(jnp.int16)


def decode(codes, steps):
    return codes[...].astype(jnp.int32).astype(jnp.float32) * steps[...]


def merge(first, second):
    peak_a, sum_a, target_a = first
    peak_b, sum_b, target_b = second
    peak = jnp.maximum(peak_a, peak_b)
    total = sum_a * jnp.exp(peak_a - peak) + sum_b * jnp.exp(peak_b - peak)
    return peak, total, target_a + target_b


def kernel(
    n, n_tensor, hidden_ref, targets_ref, head_ref, result_ref,
    other_hidden, own_rows, other_rows, outbox, inbox, outbox_steps, inbox_steps,
    group_stats, tensor_stats,
    local_sem, swap_send, swap_recv, hid_sem, ring_send, ring_recv,
    step_send, step_recv,
    group_send, group_recv, tensor_send, tensor_recv,
):
    chips = n // 2
    vocab = head_ref.shape[0]
    chunk = vocab // (4 * chips)
    sub = chunk // SUBS
    me = lax.axis_index("fsdp")
    tensor = lax.axis_index("tensor")
    core = lax.rem(me, 2)
    chip = me // 2
    side, along = lax.rem(chip, 2), chip // 2
    place = along + side * (chips - 1 - 2 * along)

    def device_at(position):
        upper = position // (chips // 2)
        at_chip = 2 * position + upper * (2 * (chips - 1 - position) + 1 - 2 * position)
        return at_chip * 2 + core

    neighbour = (
        device_at(lax.rem(place + 1, chips)),
        device_at(lax.rem(place + chips - 1, chips)),
    )
    twin = me + 1 - 2 * core

    def chunk_at(direction, step):
        if direction == 0:
            return lax.rem(place + 2 * chips - 1 - step, chips)
        return lax.rem(place + 1 + step, chips)

    def first_row(half, direction, step, part):
        block = half * (vocab // 2) + direction * (vocab // 4)
        return pl.multiple_of(block + chunk_at(direction, step) * chunk + part * sub, sub)

    def fetch(direction, step, part):
        return pltpu.make_async_copy(
            head_ref.at[pl.ds(first_row(core, direction, step, part), sub), :],
            own_rows.at[direction, step, part],
            local_sem.at[direction, step, part],
        )

    def swap(direction, step, part):
        return pltpu.make_async_remote_copy(
            src_ref=head_ref.at[pl.ds(first_row(1 - core, direction, step, part), sub), :],
            dst_ref=other_rows.at[direction, step, part],
            send_sem=swap_send.at[direction, step, part],
            recv_sem=swap_recv.at[direction, step, part],
            device_id={"fsdp": twin},
            device_id_type=MESH,
        )

    def pass_on(direction, step, part):
        slot = direction, step, part
        pairs = (
            (outbox_steps, inbox_steps, step_send, step_recv),
            (outbox, inbox, ring_send, ring_recv),
        )
        return [
            pltpu.make_async_remote_copy(
                src_ref=source.at[slot],
                dst_ref=target.at[slot],
                send_sem=send_sem.at[slot],
                recv_sem=recv_sem.at[slot],
                device_id={"fsdp": neighbour[direction]},
                device_id_type=MESH,
            )
            for source, target, send_sem, recv_sem in pairs
        ]

    def send(values, direction, step, part):
        slot = direction, step, part
        encode(values, outbox.at[slot], outbox_steps.at[slot])
        for copy in pass_on(direction, step, part):
            copy.start()

    def received(direction, step, part):
        slot = direction, step, part
        for copy in pass_on(direction, step, part):
            copy.wait_recv()
        return decode(inbox.at[slot], inbox_steps.at[slot])

    blocks = [(direction, part) for part in range(SUBS) for direction in range(2)]

    for direction, part in blocks:
        fetch(direction, 0, part).start()

    barrier = pltpu.get_barrier_semaphore()
    greeted = [{"fsdp": twin}, {"fsdp": neighbour[0]}, {"fsdp": neighbour[1]}]
    for offset in range(1, n_tensor):
        greeted.append({"tensor": lax.rem(tensor + offset, n_tensor)})
    for device in greeted:
        pl.semaphore_signal(barrier, inc=1, device_id=device, device_id_type=MESH)
    pl.semaphore_wait(barrier, len(greeted))

    hidden_swap = pltpu.make_async_remote_copy(
        src_ref=hidden_ref,
        dst_ref=other_hidden,
        send_sem=hid_sem.at[0],
        recv_sem=hid_sem.at[1],
        device_id={"fsdp": twin},
        device_id_type=MESH,
    )
    hidden_swap.start()

    for direction, part in blocks:
        swap(direction, 0, part).start()
    hidden_swap.wait_recv()

    def product(direction, step, part):
        contract = (((1,), (1,)), ((), ()))
        own = lax.dot_general(
            own_rows[direction, step, part], hidden_ref[...], contract,
            preferred_element_type=jnp.float32,
        )
        other = lax.dot_general(
            other_rows[direction, step, part], other_hidden[...], contract,
            preferred_element_type=jnp.float32,
        )
        return own + other

    def ask(step):
        for direction, part in blocks:
            fetch(direction, step, part).start()
            swap(direction, step, part).start()

    def rows_ready(direction, step, part):
        fetch(direction, step, part).wait()
        swap(direction, step, part).wait_recv()

    for direction, part in blocks:
        rows_ready(direction, 0, part)
        send(product(direction, 0, part), direction, 0, part)
    ask(1)

    @pl.loop(1, chips - 1)
    def _(step):
        ask(step + 1)
        for direction, part in blocks:
            rows_ready(direction, step, part)
            mine = product(direction, step, part)
            send(mine + received(direction, step - 1, part), direction, step, part)

    last = chips - 1
    stats = None
    tokens = hidden_ref.shape[0]
    row_ids = lax.broadcasted_iota(jnp.int32, (sub, tokens), 0)
    for direction, part in blocks:
        rows_ready(direction, last, part)
        logits = product(direction, last, part)
        logits = logits + received(direction, last - 1, part)
        start = tensor * vocab + first_row(core, direction, last, part)
        hit = row_ids + start == targets_ref[...]
        peak = jnp.max(logits, axis=0, keepdims=True)
        found = (
            peak,
            jnp.sum(jnp.exp(logits - peak), axis=0, keepdims=True),
            jnp.sum(jnp.where(hit, logits, 0.0), axis=0, keepdims=True),
        )
        stats = found if stats is None else merge(stats, found)

    def exchange(axis, size, index, slots, send_sem, recv_sem):
        def give(offset):
            return pltpu.make_async_remote_copy(
                src_ref=slots.at[index],
                dst_ref=slots.at[index],
                send_sem=send_sem.at[offset],
                recv_sem=recv_sem.at[index],
                device_id={axis: lax.rem(index + offset, size)},
                device_id_type=MESH,
            )

        def take(offset):
            source = lax.rem(index + offset, size)
            return pltpu.make_async_remote_copy(
                src_ref=slots.at[source],
                dst_ref=slots.at[source],
                send_sem=send_sem.at[offset],
                recv_sem=recv_sem.at[source],
                device_id={axis: source},
                device_id_type=MESH,
            )

        @pl.loop(1, size)
        def _(offset):
            give(offset).start()

        @pl.loop(1, size)
        def _(offset):
            take(offset).wait_recv()

        peaks = slots[:, 0:lines, :]
        peak = jnp.max(peaks, axis=0)
        total = jnp.sum(slots[:, lines : 2 * lines, :] * jnp.exp(peaks - peak), axis=0)
        target = jnp.sum(slots[:, 2 * lines : 3 * lines, :], axis=0)

        def finish():
            @pl.loop(1, size)
            def _(offset):
                give(offset).wait_send()

        return (peak, total, target), finish

    lanes = group_stats.shape[2]
    lines = tokens // lanes
    group_stats[me] = jnp.zeros(group_stats.shape[1:], jnp.float32)
    for which in range(3):
        for line in range(lines):
            group_stats[me, which * lines + line : which * lines + line + 1, :] = stats[which][
                :, line * lanes : (line + 1) * lanes
            ]
    stats, finish_group = exchange("fsdp", n, me, group_stats, group_send, group_recv)
    tensor_stats[tensor] = jnp.zeros(tensor_stats.shape[1:], jnp.float32)
    for which in range(3):
        tensor_stats[tensor, which * lines : (which + 1) * lines, :] = stats[which]
    stats, finish_tensor = exchange(
        "tensor", n_tensor, tensor, tensor_stats, tensor_send, tensor_recv
    )

    peak, total, target = stats
    gap = target - peak
    result_ref[0] = gap - jnp.log(total)
    result_ref[1] = gap

    finish_group()
    finish_tensor()
    hidden_swap.wait_send()

    @pl.loop(0, chips)
    def _(step):
        for direction, part in blocks:
            swap(direction, step, part).wait_send()

    @pl.loop(0, chips - 1)
    def _(step):
        for direction, part in blocks:
            for copy in pass_on(direction, step, part):
                copy.wait_send()


def solution(mesh):
    n, n_tensor = mesh.shape["fsdp"], mesh.shape["tensor"]

    def per_device(hidden, head_weight, targets):
        tokens, depth = hidden.shape
        vocab = head_weight.shape[0]
        chips = n // 2
        chunk = vocab // (4 * chips)
        sub = chunk // SUBS
        lanes = min(tokens, 128)
        lines = tokens // lanes
        slot_rows = -(-3 * lines // 8) * 8
        vmem = pl.BlockSpec(memory_space=pltpu.VMEM)
        dma = pltpu.SemaphoreType.DMA
        result = pl.pallas_call(
            functools.partial(kernel, n, n_tensor),
            out_shape=jax.ShapeDtypeStruct((2, lines, lanes), jnp.float32),
            in_specs=[vmem, vmem, pl.BlockSpec(memory_space=pl.ANY)],
            out_specs=vmem,
            scratch_shapes=[
                pltpu.VMEM((tokens, depth), hidden.dtype),
                pltpu.VMEM((2, chips, SUBS, sub, depth), head_weight.dtype),
                pltpu.VMEM((2, chips, SUBS, sub, depth), head_weight.dtype),
                pltpu.VMEM((2, chips - 1, SUBS, sub, tokens), jnp.int16),
                pltpu.VMEM((2, chips - 1, SUBS, sub, tokens), jnp.int16),
                pltpu.VMEM((2, chips - 1, SUBS, 1, tokens), jnp.float32),
                pltpu.VMEM((2, chips - 1, SUBS, 1, tokens), jnp.float32),
                pltpu.VMEM((n, slot_rows, lanes), jnp.float32),
                pltpu.VMEM((n_tensor, slot_rows, lanes), jnp.float32),
                dma((2, chips, SUBS)),
                dma((2, chips, SUBS)),
                dma((2, chips, SUBS)),
                dma((2,)),
                dma((2, chips - 1, SUBS)),
                dma((2, chips - 1, SUBS)),
                dma((2, chips - 1, SUBS)),
                dma((2, chips - 1, SUBS)),
                dma((n,)),
                dma((n,)),
                dma((n_tensor,)),
                dma((n_tensor,)),
            ],
            compiler_params=pltpu.CompilerParams(
                collective_id=0, has_side_effects=True, vmem_limit_bytes=60 * 1024 * 1024
            ),
        )(hidden, targets.reshape(1, tokens), head_weight)
        return result[0].reshape(tokens), result[1].reshape(tokens)

    return jax.shard_map(
        per_device,
        mesh=mesh,
        in_specs=(P(None, "fsdp"), P("tensor", "fsdp"), P()),
        out_specs=(P(), P()),
        check_vma=False,
    )
```

```python
import functools

import jax
import jax.numpy as jnp
from jax import lax
from jax.experimental import pallas as pl
from jax.experimental.pallas import tpu as pltpu
from jax.sharding import PartitionSpec as P

MESH = pl.DeviceIdType.MESH
TOP_CODE = 32700.0
SUBS = 4


def encode(values, codes, steps):
    largest = jnp.maximum(jnp.max(jnp.abs(values), axis=0, keepdims=True), 1e-30)
    steps[...] = largest * (1.0 / TOP_CODE)
    scaled = jnp.floor(values * (TOP_CODE / largest) + 0.5)
    codes[...] = scaled.astype(jnp.int32).astype(jnp.int16)


def decode(codes, steps):
    return codes[...].astype(jnp.int32).astype(jnp.float32) * steps[...]


def merge(first, second):
    peak_a, sum_a, target_a = first
    peak_b, sum_b, target_b = second
    peak = jnp.maximum(peak_a, peak_b)
    total = sum_a * jnp.exp(peak_a - peak) + sum_b * jnp.exp(peak_b - peak)
    return peak, total, target_a + target_b


def kernel(
    n, n_tensor, hidden_ref, targets_ref, head_ref, result_ref,
    other_hidden, own_rows, other_rows, outbox, inbox, outbox_steps, inbox_steps,
    group_stats, tensor_stats,
    local_sem, swap_send, swap_recv, hid_sem, ring_send, ring_recv,
    step_send, step_recv,
    group_send, group_recv, tensor_send, tensor_recv,
):
    chips = n // 2
    vocab = head_ref.shape[0]
    chunk = vocab // (4 * chips)
    sub = chunk // SUBS
    me = lax.axis_index("fsdp")
    tensor = lax.axis_index("tensor")
    core = lax.rem(me, 2)
    chip = me // 2
    side, along = lax.rem(chip, 2), chip // 2
    place = along + side * (chips - 1 - 2 * along)

    def device_at(position):
        upper = position // (chips // 2)
        at_chip = 2 * position + upper * (2 * (chips - 1 - position) + 1 - 2 * position)
        return at_chip * 2 + core

    neighbour = (
        device_at(lax.rem(place + 1, chips)),
        device_at(lax.rem(place + chips - 1, chips)),
    )
    twin = me + 1 - 2 * core

    def chunk_at(direction, step):
        if direction == 0:
            return lax.rem(place + 2 * chips - 1 - step, chips)
        return lax.rem(place + 1 + step, chips)

    def first_row(half, direction, step, part):
        block = half * (vocab // 2) + direction * (vocab // 4)
        return pl.multiple_of(block + chunk_at(direction, step) * chunk + part * sub, sub)

    def fetch(direction, step, part):
        return pltpu.make_async_copy(
            head_ref.at[pl.ds(first_row(core, direction, step, part), sub), :],
            own_rows.at[direction, step, part],
            local_sem.at[direction, step, part],
        )

    def swap(direction, step, part):
        return pltpu.make_async_remote_copy(
            src_ref=head_ref.at[pl.ds(first_row(1 - core, direction, step, part), sub), :],
            dst_ref=other_rows.at[direction, step, part],
            send_sem=swap_send.at[direction, step, part],
            recv_sem=swap_recv.at[direction, step, part],
            device_id={"fsdp": twin},
            device_id_type=MESH,
        )

    def pass_on(direction, step, part):
        slot = direction, step, part
        pairs = (
            (outbox_steps, inbox_steps, step_send, step_recv),
            (outbox, inbox, ring_send, ring_recv),
        )
        return [
            pltpu.make_async_remote_copy(
                src_ref=source.at[slot],
                dst_ref=target.at[slot],
                send_sem=send_sem.at[slot],
                recv_sem=recv_sem.at[slot],
                device_id={"fsdp": neighbour[direction]},
                device_id_type=MESH,
            )
            for source, target, send_sem, recv_sem in pairs
        ]

    def send(values, direction, step, part):
        slot = direction, step, part
        encode(values, outbox.at[slot], outbox_steps.at[slot])
        for copy in pass_on(direction, step, part):
            copy.start()

    def received(direction, step, part):
        slot = direction, step, part
        for copy in pass_on(direction, step, part):
            copy.wait_recv()
        return decode(inbox.at[slot], inbox_steps.at[slot])

    blocks = [(direction, part) for part in range(SUBS) for direction in range(2)]

    for direction, part in blocks:
        fetch(direction, 0, part).start()

    barrier = pltpu.get_barrier_semaphore()
    greeted = [{"fsdp": twin}, {"fsdp": neighbour[0]}, {"fsdp": neighbour[1]}]
    for offset in range(1, n_tensor):
        greeted.append({"tensor": lax.rem(tensor + offset, n_tensor)})
    for device in greeted:
        pl.semaphore_signal(barrier, inc=1, device_id=device, device_id_type=MESH)
    pl.semaphore_wait(barrier, len(greeted))

    hidden_swap = pltpu.make_async_remote_copy(
        src_ref=hidden_ref,
        dst_ref=other_hidden,
        send_sem=hid_sem.at[0],
        recv_sem=hid_sem.at[1],
        device_id={"fsdp": twin},
        device_id_type=MESH,
    )
    hidden_swap.start()

    for direction, part in blocks:
        swap(direction, 0, part).start()
    hidden_swap.wait_recv()

    def product(direction, step, part):
        contract = (((1,), (1,)), ((), ()))
        own = lax.dot_general(
            own_rows[direction, step, part], hidden_ref[...], contract,
            preferred_element_type=jnp.float32,
        )
        other = lax.dot_general(
            other_rows[direction, step, part], other_hidden[...], contract,
            preferred_element_type=jnp.float32,
        )
        return own + other

    def ask(step):
        for direction, part in blocks:
            fetch(direction, step, part).start()
            swap(direction, step, part).start()

    def rows_ready(direction, step, part):
        fetch(direction, step, part).wait()
        swap(direction, step, part).wait_recv()

    for direction, part in blocks:
        rows_ready(direction, 0, part)
        send(product(direction, 0, part), direction, 0, part)
    ask(1)

    @pl.loop(1, chips - 1)
    def _(step):
        ask(step + 1)
        for direction, part in blocks:
            rows_ready(direction, step, part)
            mine = product(direction, step, part)
            send(mine + received(direction, step - 1, part), direction, step, part)

    last = chips - 1
    stats = None
    tokens = hidden_ref.shape[0]
    row_ids = lax.broadcasted_iota(jnp.int32, (sub, tokens), 0)
    for direction, part in blocks:
        rows_ready(direction, last, part)
        logits = product(direction, last, part)
        logits = logits + received(direction, last - 1, part)
        start = tensor * vocab + first_row(core, direction, last, part)
        hit = row_ids + start == targets_ref[...]
        peak = jnp.max(logits, axis=0, keepdims=True)
        found = (
            peak,
            jnp.sum(jnp.exp(logits - peak), axis=0, keepdims=True),
            jnp.sum(jnp.where(hit, logits, 0.0), axis=0, keepdims=True),
        )
        stats = found if stats is None else merge(stats, found)

    def drain():
        hidden_swap.wait_send()

        @pl.loop(0, chips)
        def _(step):
            for direction, part in blocks:
                swap(direction, step, part).wait_send()

        @pl.loop(0, chips - 1)
        def _(step):
            for direction, part in blocks:
                for copy in pass_on(direction, step, part):
                    copy.wait_send()

    def exchange(axis, size, index, slots, send_sem, recv_sem, meanwhile):
        def give(offset):
            return pltpu.make_async_remote_copy(
                src_ref=slots.at[index],
                dst_ref=slots.at[index],
                send_sem=send_sem.at[offset],
                recv_sem=recv_sem.at[index],
                device_id={axis: lax.rem(index + offset, size)},
                device_id_type=MESH,
            )

        def take(offset):
            source = lax.rem(index + offset, size)
            return pltpu.make_async_remote_copy(
                src_ref=slots.at[source],
                dst_ref=slots.at[source],
                send_sem=send_sem.at[offset],
                recv_sem=recv_sem.at[source],
                device_id={axis: source},
                device_id_type=MESH,
            )

        @pl.loop(1, size)
        def _(offset):
            give(offset).start()

        meanwhile()

        @pl.loop(1, size)
        def _(offset):
            take(offset).wait_recv()

        peaks = slots[:, 0:lines, :]
        peak = jnp.max(peaks, axis=0)
        total = jnp.sum(slots[:, lines : 2 * lines, :] * jnp.exp(peaks - peak), axis=0)
        target = jnp.sum(slots[:, 2 * lines : 3 * lines, :], axis=0)

        def finish():
            @pl.loop(1, size)
            def _(offset):
                give(offset).wait_send()

        return (peak, total, target), finish

    lanes = group_stats.shape[2]
    lines = tokens // lanes
    group_stats[me] = jnp.zeros(group_stats.shape[1:], jnp.float32)
    for which in range(3):
        for line in range(lines):
            group_stats[me, which * lines + line : which * lines + line + 1, :] = stats[which][
                :, line * lanes : (line + 1) * lanes
            ]
    stats, finish_group = exchange(
        "fsdp", n, me, group_stats, group_send, group_recv, drain
    )
    tensor_stats[tensor] = jnp.zeros(tensor_stats.shape[1:], jnp.float32)
    for which in range(3):
        tensor_stats[tensor, which * lines : (which + 1) * lines, :] = stats[which]
    stats, finish_tensor = exchange(
        "tensor", n_tensor, tensor, tensor_stats, tensor_send, tensor_recv, finish_group
    )

    peak, total, target = stats
    gap = target - peak
    result_ref[0] = gap - jnp.log(total)
    result_ref[1] = gap

    finish_tensor()


def solution(mesh):
    n, n_tensor = mesh.shape["fsdp"], mesh.shape["tensor"]

    def per_device(hidden, head_weight, targets):
        tokens, depth = hidden.shape
        vocab = head_weight.shape[0]
        chips = n // 2
        chunk = vocab // (4 * chips)
        sub = chunk // SUBS
        lanes = min(tokens, 128)
        lines = tokens // lanes
        slot_rows = -(-3 * lines // 8) * 8
        vmem = pl.BlockSpec(memory_space=pltpu.VMEM)
        dma = pltpu.SemaphoreType.DMA
        result = pl.pallas_call(
            functools.partial(kernel, n, n_tensor),
            out_shape=jax.ShapeDtypeStruct((2, lines, lanes), jnp.float32),
            in_specs=[vmem, vmem, pl.BlockSpec(memory_space=pl.ANY)],
            out_specs=vmem,
            scratch_shapes=[
                pltpu.VMEM((tokens, depth), hidden.dtype),
                pltpu.VMEM((2, chips, SUBS, sub, depth), head_weight.dtype),
                pltpu.VMEM((2, chips, SUBS, sub, depth), head_weight.dtype),
                pltpu.VMEM((2, chips - 1, SUBS, sub, tokens), jnp.int16),
                pltpu.VMEM((2, chips - 1, SUBS, sub, tokens), jnp.int16),
                pltpu.VMEM((2, chips - 1, SUBS, 1, tokens), jnp.float32),
                pltpu.VMEM((2, chips - 1, SUBS, 1, tokens), jnp.float32),
                pltpu.VMEM((n, slot_rows, lanes), jnp.float32),
                pltpu.VMEM((n_tensor, slot_rows, lanes), jnp.float32),
                dma((2, chips, SUBS)),
                dma((2, chips, SUBS)),
                dma((2, chips, SUBS)),
                dma((2,)),
                dma((2, chips - 1, SUBS)),
                dma((2, chips - 1, SUBS)),
                dma((2, chips - 1, SUBS)),
                dma((2, chips - 1, SUBS)),
                dma((n,)),
                dma((n,)),
                dma((n_tensor,)),
                dma((n_tensor,)),
            ],
            compiler_params=pltpu.CompilerParams(
                collective_id=0, has_side_effects=True, vmem_limit_bytes=60 * 1024 * 1024
            ),
        )(hidden, targets.reshape(1, tokens), head_weight)
        return result[0].reshape(tokens), result[1].reshape(tokens)

    return jax.shard_map(
        per_device,
        mesh=mesh,
        in_specs=(P(None, "fsdp"), P("tensor", "fsdp"), P()),
        out_specs=(P(), P()),
        check_vma=False,
    )
```

```python
import functools

import jax
import jax.numpy as jnp
from jax import lax
from jax.experimental import pallas as pl
from jax.experimental.pallas import tpu as pltpu
from jax.sharding import PartitionSpec as P

MESH = pl.DeviceIdType.MESH
TOP_CODE = 32700.0
SUBS = 2


def encode(values, codes, steps):
    largest = jnp.maximum(jnp.max(jnp.abs(values), axis=0, keepdims=True), 1e-30)
    steps[...] = largest * (1.0 / TOP_CODE)
    scaled = jnp.floor(values * (TOP_CODE / largest) + 0.5)
    codes[...] = scaled.astype(jnp.int32).astype(jnp.int16)


def decode(codes, steps):
    return codes[...].astype(jnp.int32).astype(jnp.float32) * steps[...]


def merge(first, second):
    peak_a, sum_a, target_a = first
    peak_b, sum_b, target_b = second
    peak = jnp.maximum(peak_a, peak_b)
    total = sum_a * jnp.exp(peak_a - peak) + sum_b * jnp.exp(peak_b - peak)
    return peak, total, target_a + target_b


def kernel(
    n, n_tensor, hidden_ref, targets_ref, head_ref, result_ref,
    other_hidden, own_rows, other_rows, outbox, inbox, outbox_steps, inbox_steps,
    group_stats, tensor_stats,
    local_sem, swap_send, swap_recv, hid_sem, ring_send, ring_recv,
    step_send, step_recv,
    group_send, group_recv, tensor_send, tensor_recv,
):
    chips = n // 2
    vocab = head_ref.shape[0]
    chunk = vocab // (4 * chips)
    sub = chunk // SUBS
    me = lax.axis_index("fsdp")
    tensor = lax.axis_index("tensor")
    core = lax.rem(me, 2)
    chip = me // 2
    side, along = lax.rem(chip, 2), chip // 2
    place = along + side * (chips - 1 - 2 * along)

    def device_at(position):
        upper = position // (chips // 2)
        at_chip = 2 * position + upper * (2 * (chips - 1 - position) + 1 - 2 * position)
        return at_chip * 2 + core

    def neighbour(direction):
        return device_at(lax.rem(place + 1 + direction * (chips - 2), chips))

    twin = me + 1 - 2 * core

    def chunk_at(direction, step):
        return lax.rem(place + 2 * chips + (2 * direction - 1) * (1 + step), chips)

    def first_row(half, direction, step, part):
        block = half * (vocab // 2) + direction * (vocab // 4)
        return pl.multiple_of(block + chunk_at(direction, step) * chunk + part * sub, sub)

    def fetch(direction, step, part):
        return pltpu.make_async_copy(
            head_ref.at[pl.ds(first_row(core, direction, step, part), sub), :],
            own_rows.at[direction, step, part],
            local_sem.at[direction, step, part],
        )

    def swap(direction, step, part):
        return pltpu.make_async_remote_copy(
            src_ref=head_ref.at[pl.ds(first_row(1 - core, direction, step, part), sub), :],
            dst_ref=other_rows.at[direction, step, part],
            send_sem=swap_send.at[direction, step, part],
            recv_sem=swap_recv.at[direction, step, part],
            device_id={"fsdp": twin},
            device_id_type=MESH,
        )

    def pass_on(direction, step, part):
        slot = direction, step, part
        pairs = (
            (outbox_steps, inbox_steps, step_send, step_recv),
            (outbox, inbox, ring_send, ring_recv),
        )
        return [
            pltpu.make_async_remote_copy(
                src_ref=source.at[slot],
                dst_ref=target.at[slot],
                send_sem=send_sem.at[slot],
                recv_sem=recv_sem.at[slot],
                device_id={"fsdp": neighbour(direction)},
                device_id_type=MESH,
            )
            for source, target, send_sem, recv_sem in pairs
        ]

    def send(values, direction, step, part):
        slot = direction, step, part
        encode(values, outbox.at[slot], outbox_steps.at[slot])
        for copy in pass_on(direction, step, part):
            copy.start()

    def received(direction, step, part):
        slot = direction, step, part
        for copy in pass_on(direction, step, part):
            copy.wait_recv()
        return decode(inbox.at[slot], inbox_steps.at[slot])

    blocks = [(lax.rem(core + turn, 2), part) for part in range(SUBS) for turn in range(2)]

    for direction, part in blocks:
        fetch(direction, 0, part).start()

    barrier = pltpu.get_barrier_semaphore()
    greeted = [{"fsdp": twin}, {"fsdp": neighbour(0)}, {"fsdp": neighbour(1)}]
    for offset in range(1, n_tensor):
        greeted.append({"tensor": lax.rem(tensor + offset, n_tensor)})
    for device in greeted:
        pl.semaphore_signal(barrier, inc=1, device_id=device, device_id_type=MESH)
    pl.semaphore_wait(barrier, len(greeted))

    hidden_swap = pltpu.make_async_remote_copy(
        src_ref=hidden_ref,
        dst_ref=other_hidden,
        send_sem=hid_sem.at[0],
        recv_sem=hid_sem.at[1],
        device_id={"fsdp": twin},
        device_id_type=MESH,
    )
    hidden_swap.start()

    for direction, part in blocks:
        swap(direction, 0, part).start()
    hidden_swap.wait_recv()

    def product(direction, step, part):
        contract = (((1,), (1,)), ((), ()))
        own = lax.dot_general(
            own_rows[direction, step, part], hidden_ref[...], contract,
            preferred_element_type=jnp.float32,
        )
        other = lax.dot_general(
            other_rows[direction, step, part], other_hidden[...], contract,
            preferred_element_type=jnp.float32,
        )
        return own + other

    def ask(step):
        for direction, part in blocks:
            fetch(direction, step, part).start()
            swap(direction, step, part).start()

    def rows_ready(direction, step, part):
        fetch(direction, step, part).wait()
        swap(direction, step, part).wait_recv()

    for direction, part in blocks:
        rows_ready(direction, 0, part)
        send(product(direction, 0, part), direction, 0, part)
    ask(1)

    @pl.loop(1, chips - 1)
    def _(step):
        ask(step + 1)
        for direction, part in blocks:
            rows_ready(direction, step, part)
            mine = product(direction, step, part)
            send(mine + received(direction, step - 1, part), direction, step, part)

    last = chips - 1
    stats = None
    tokens = hidden_ref.shape[0]
    row_ids = lax.broadcasted_iota(jnp.int32, (sub, tokens), 0)
    for direction, part in blocks:
        rows_ready(direction, last, part)
        logits = product(direction, last, part)
        logits = logits + received(direction, last - 1, part)
        start = tensor * vocab + first_row(core, direction, last, part)
        hit = row_ids + start == targets_ref[...]
        peak = jnp.max(logits, axis=0, keepdims=True)
        found = (
            peak,
            jnp.sum(jnp.exp(logits - peak), axis=0, keepdims=True),
            jnp.sum(jnp.where(hit, logits, 0.0), axis=0, keepdims=True),
        )
        stats = found if stats is None else merge(stats, found)

    def drain():
        hidden_swap.wait_send()

        @pl.loop(0, chips)
        def _(step):
            for direction, part in blocks:
                swap(direction, step, part).wait_send()

        @pl.loop(0, chips - 1)
        def _(step):
            for direction, part in blocks:
                for copy in pass_on(direction, step, part):
                    copy.wait_send()

    def exchange(axis, size, index, slots, send_sem, recv_sem, meanwhile):
        def give(offset):
            return pltpu.make_async_remote_copy(
                src_ref=slots.at[index],
                dst_ref=slots.at[index],
                send_sem=send_sem.at[offset],
                recv_sem=recv_sem.at[index],
                device_id={axis: lax.rem(index + offset, size)},
                device_id_type=MESH,
            )

        def take(offset):
            source = lax.rem(index + offset, size)
            return pltpu.make_async_remote_copy(
                src_ref=slots.at[source],
                dst_ref=slots.at[source],
                send_sem=send_sem.at[offset],
                recv_sem=recv_sem.at[source],
                device_id={axis: source},
                device_id_type=MESH,
            )

        @pl.loop(1, size)
        def _(offset):
            give(offset).start()

        meanwhile()

        @pl.loop(1, size)
        def _(offset):
            take(offset).wait_recv()

        peaks = slots[:, 0:lines, :]
        peak = jnp.max(peaks, axis=0)
        total = jnp.sum(slots[:, lines : 2 * lines, :] * jnp.exp(peaks - peak), axis=0)
        target = jnp.sum(slots[:, 2 * lines : 3 * lines, :], axis=0)

        def finish():
            @pl.loop(1, size)
            def _(offset):
                give(offset).wait_send()

        return (peak, total, target), finish

    lanes = group_stats.shape[2]
    lines = tokens // lanes
    group_stats[me] = jnp.zeros(group_stats.shape[1:], jnp.float32)
    for which in range(3):
        for line in range(lines):
            group_stats[me, which * lines + line : which * lines + line + 1, :] = stats[which][
                :, line * lanes : (line + 1) * lanes
            ]
    stats, finish_group = exchange(
        "fsdp", n, me, group_stats, group_send, group_recv, drain
    )
    tensor_stats[tensor] = jnp.zeros(tensor_stats.shape[1:], jnp.float32)
    for which in range(3):
        tensor_stats[tensor, which * lines : (which + 1) * lines, :] = stats[which]
    stats, finish_tensor = exchange(
        "tensor", n_tensor, tensor, tensor_stats, tensor_send, tensor_recv, finish_group
    )

    peak, total, target = stats
    gap = target - peak
    result_ref[0] = gap - jnp.log(total)
    result_ref[1] = gap

    finish_tensor()


def solution(mesh):
    n, n_tensor = mesh.shape["fsdp"], mesh.shape["tensor"]

    def per_device(hidden, head_weight, targets):
        tokens, depth = hidden.shape
        vocab = head_weight.shape[0]
        chips = n // 2
        chunk = vocab // (4 * chips)
        sub = chunk // SUBS
        lanes = min(tokens, 128)
        lines = tokens // lanes
        slot_rows = -(-3 * lines // 8) * 8
        vmem = pl.BlockSpec(memory_space=pltpu.VMEM)
        dma = pltpu.SemaphoreType.DMA
        result = pl.pallas_call(
            functools.partial(kernel, n, n_tensor),
            out_shape=jax.ShapeDtypeStruct((2, lines, lanes), jnp.float32),
            in_specs=[vmem, vmem, pl.BlockSpec(memory_space=pl.ANY)],
            out_specs=vmem,
            scratch_shapes=[
                pltpu.VMEM((tokens, depth), hidden.dtype),
                pltpu.VMEM((2, chips, SUBS, sub, depth), head_weight.dtype),
                pltpu.VMEM((2, chips, SUBS, sub, depth), head_weight.dtype),
                pltpu.VMEM((2, chips - 1, SUBS, sub, tokens), jnp.int16),
                pltpu.VMEM((2, chips - 1, SUBS, sub, tokens), jnp.int16),
                pltpu.VMEM((2, chips - 1, SUBS, 1, tokens), jnp.float32),
                pltpu.VMEM((2, chips - 1, SUBS, 1, tokens), jnp.float32),
                pltpu.VMEM((n, slot_rows, lanes), jnp.float32),
                pltpu.VMEM((n_tensor, slot_rows, lanes), jnp.float32),
                dma((2, chips, SUBS)),
                dma((2, chips, SUBS)),
                dma((2, chips, SUBS)),
                dma((2,)),
                dma((2, chips - 1, SUBS)),
                dma((2, chips - 1, SUBS)),
                dma((2, chips - 1, SUBS)),
                dma((2, chips - 1, SUBS)),
                dma((n,)),
                dma((n,)),
                dma((n_tensor,)),
                dma((n_tensor,)),
            ],
            compiler_params=pltpu.CompilerParams(
                collective_id=0, has_side_effects=True, vmem_limit_bytes=60 * 1024 * 1024
            ),
        )(hidden, targets.reshape(1, tokens), head_weight)
        return result[0].reshape(tokens), result[1].reshape(tokens)

    return jax.shard_map(
        per_device,
        mesh=mesh,
        in_specs=(P(None, "fsdp"), P("tensor", "fsdp"), P()),
        out_specs=(P(), P()),
        check_vma=False,
    )
```
